256 devices in a mesh: ep: 64 (over z, x, core), tp: 4 (over y).
Axes of the slice: x: 4, y: 4, z: 8, core: 2. Of those that a mesh axis runs over, the one named last changes fastest.
Arguments:
- hidden_in: bfloat16 [8192, 2048], P('ep', 'tp'), may hold values from -50 to 50
- norm_gain: float32 [2048], P('tp'), may hold values from 0.5 to 1.5
- expert_ids: int32 [8192, 8], P('ep'), may hold values from 0 to 127, all different within a row; in each aligned block of 128 rows (0 to 127, 128 to 255, ...) at most 12 rows name the same one
- routing_weight: float32 [8192, 8], P('ep'), may hold values from 0.03 to 0.3
- labels: int32 [8192], P('ep'), may hold values from 0 to 3
- grad_later: bfloat16 [8192, 2048], P('ep', 'tp'), may hold values from -6 to 6
- head_weight: bfloat16 [2048, 4], P('tp'), may hold values from -0.125 to 0.125
- gate_weight: bfloat16 [98304, 2048], P(('ep', 'tp')), may hold values from -0.125 to 0.125
- up_weight: bfloat16 [98304, 2048], P(('ep', 'tp')), may hold values from -0.125 to 0.125
- down_weight: bfloat16 [98304, 2048], P(('ep', 'tp')), may hold values from -0.21875 to 0.21875
Outputs:
- token_loss: float32 [8192], P('ep')
- outcome: bfloat16 [8192, 2048], P('ep', 'tp')
- grad_input: bfloat16 [8192, 2048], P('ep', 'tp')
- grad_gate: bfloat16 [98304, 2048], P(('ep', 'tp'))
- grad_up: bfloat16 [98304, 2048], P(('ep', 'tp'))
- grad_down: bfloat16 [98304, 2048], P(('ep', 'tp'))
The draws below stay inside these ranges and needn't reach their ends.
Inputs may be any that keep to these rules, and one draw needn't show every extreme that they name: `expert_ids`: each row names 8 different experts. Within the 128 rows of one index of ep, no expert is named more than 12 times, a bound that some block reaches.
All inputs are finite; a program needn't handle non-finite values.
Results may differ from the reference program's by a relative error of at most 0.011.
Values may be sent and summed in bfloat16 or wider, within the bound.
A program may use at most 128 MiB of HBM per device.

```python
import math
import jax
import jax.numpy as jnp
import numpy as np
from jax import lax

D = 2048
FF = 768
TOP = 8
LABELS = 4
TOK_DEV = 128
EXPERTS = 128
UNITS = 384
CAP = 12
TOKENS = 8192
N_EP = 64


def draw_hidden_in(key, part):
    key_base, key_row, key_col = jax.random.split(key, 3)
    position = jnp.arange(D, dtype=jnp.float32) / D
    base = jnp.clip(jax.random.normal(key_base, (TOKENS, D), jnp.float32), -5.0, 5.0)
    row_scale = jnp.exp(jax.random.uniform(key_row, (TOKENS, 1), jnp.float32, 0.0, math.log(10.0))) / 3.0
    col_scale = jnp.exp(jax.random.uniform(key_col, (1, D), jnp.float32, 0.0, math.log(10.0))) * (3.0 ** position)[None, :]
    return (base * row_scale * col_scale / 12.0).astype(jnp.bfloat16)


def plant(drawn, rng, low, largest):
    extent = drawn.shape
    index_at = [jax.random.randint(jax.random.fold_in(rng, axis), (), 0, extent[axis]) for axis in range(len(extent))]
    drawn = drawn.at[tuple(index_at)].set(low)
    longest = extent.index(max(extent))
    index_at[longest] = (index_at[longest] + 1) % extent[longest]
    return drawn.at[tuple(index_at)].set(largest)


def block_scale(own_key, dims, cuts, smallest, high):
    level, own = 1.0, jax.random.fold_in(own_key, 6)
    for dim, blocks in cuts:
        heights = jnp.exp(jax.random.uniform(jax.random.fold_in(own, dim), (blocks,), jnp.float32, smallest / len(cuts), high / len(cuts)))
        level = level * jnp.repeat(heights, dims[dim] // blocks).reshape([-1 if axis == dim else 1 for axis in range(len(dims))])
    return level


def assign_block(rng, own, number, rows, number_of, top, reach, skew):
    order = jax.random.permutation(rng, number_of)
    crowded, usual = load_shares(number_of, rows * top, reach, skew, True), load_shares(number_of, rows * top, reach, skew, False)
    places = jnp.arange(number_of)

    def named(sizes, turn):
        used = int((sizes > 0).sum())
        fixed = max(1, used // 4)
        shifted = fixed + (places - fixed + turn * (used - fixed)) % max(1, number_of - fixed)
        return jnp.zeros((number_of,), jnp.int32).at[order[jnp.where(places < fixed, places, shifted)]].set(jnp.asarray(sizes, jnp.int32))

    sizes = jnp.where(number % 4 == 0, named(crowded, number // 4), named(usual, number - number // 4 - 1))
    mixed = jax.random.permutation(jax.random.fold_in(own, 3), number_of)
    giver, receiver = mixed[0:number_of // 2 * 2:2], mixed[1:number_of // 2 * 2:2]
    room = jnp.minimum(sizes[giver] - 1, reach - sizes[receiver]) // 2
    room = jnp.where((giver == order[0]) | (receiver == order[0]) | (sizes[receiver] == 0), 0, jnp.maximum(room, 0))
    shifted = jax.random.randint(jax.random.fold_in(own, 4), (number_of // 2,), 0, 1 << 20) % (room + 1)
    sizes = sizes.at[giver].add(-shifted).at[receiver].add(shifted)
    items = jnp.searchsorted(jnp.cumsum(sizes), jnp.arange(rows * top), side="right").astype(jnp.int32)
    grid = items.reshape(top, rows).T
    grid = grid[jax.random.permutation(jax.random.fold_in(own, 1), rows)]
    turn = jax.random.randint(jax.random.fold_in(own, 2), (rows, 1), 0, top)
    return jnp.take_along_axis(grid, (jnp.arange(top)[None, :] + turn) % top, axis=1)


def load_shares(count, total, limit, skew, full):
    loads = [(1 << 20) // math.isqrt(rank ** skew) + 1 for rank in range(1, count + 1)]
    largest = limit if full else min(limit, max(-(-total // count), total * loads[0] // sum(loads)))
    least = 1 if total - largest >= count - 1 else 0
    holding, rest = [largest] + [least] * (count - 1), total - largest - least * (count - 1)
    while rest > 0:
        candidates = [i for i in range(1, count) if holding[i] < largest] or [i for i in range(1, count) if holding[i] < limit]
        mass, left = sum([loads[i] for i in candidates]), rest
        for i in candidates:
            addition = min(limit - holding[i], max(1, left * loads[i] // mass), rest)
            holding[i] = holding[i] + addition
            rest = rest - addition
    return np.array(holding)


def normal_values(stream_key, extent, deviation, bound, cuts=(), kind=jnp.bfloat16):
    entries = jax.random.normal(stream_key, extent, jnp.float32) * deviation
    if len(cuts) > 0:
        entries = block_scale(stream_key, extent, cuts, -0.22, 0.18) * entries
    return jnp.clip(entries, min=-bound, max=bound).astype(kind)


def setup_inputs(seed: int = 0) -> dict:
    splits = jax.random.split(jax.random.key(seed), 11)
    hidden_in = draw_hidden_in(jax.random.fold_in(splits[10], 71), 0)
    norm_gain = jnp.clip(1.0 + 0.1 * jax.random.normal(splits[1], (D,), jnp.float32), 0.5, 1.5)
    expert_ids_keys = jax.random.split(jax.random.fold_in(splits[2], 1), TOKENS // TOK_DEV)
    expert_ids_turns = jax.random.permutation(jax.random.fold_in(splits[2], 3), TOKENS // TOK_DEV)
    expert_ids = jax.vmap(lambda own, number: assign_block(jax.random.fold_in(splits[2], 2), own, number, TOK_DEV, EXPERTS, TOP, CAP, 2))(expert_ids_keys, expert_ids_turns).reshape((TOKENS, TOP))
    routing_weight = jnp.clip(jnp.exp(math.log(0.3) - 2.3025852 * jax.random.uniform(splits[3], (TOKENS, TOP), jnp.float32) ** block_scale(splits[3], (TOKENS, TOP), ((0, 64),), -0.2, 0.2)), 0.03, 0.3)
    labels = plant(jax.random.randint(splits[4], (TOKENS,), 0, LABELS), jax.random.fold_in(splits[4], 1), 0, LABELS - 1).astype(jnp.int32)
    grad_later = normal_values(splits[5], (TOKENS, D), 1.0, 6.0, ((0, 64), (1, 4)))
    head_weight = normal_values(splits[6], (D, LABELS), D ** -0.5, 0.125, ((0, 4),))
    gate_weight = normal_values(splits[7], (EXPERTS * FF, D), D ** -0.5, 0.125, ((0, 256),))
    up_weight = normal_values(splits[8], (EXPERTS * FF, D), D ** -0.5, 0.125, ((0, 256),))
    down_weight = normal_values(splits[9], (EXPERTS * FF, D), FF ** -0.5, 0.21875, ((0, 256),))
    return {"hidden_in": hidden_in, "norm_gain": norm_gain, "expert_ids": expert_ids, "routing_weight": routing_weight, "labels": labels, "grad_later": grad_later, "head_weight": head_weight, "gate_weight": gate_weight, "up_weight": up_weight, "down_weight": down_weight}


EPS = 1e-06
LOSS_SCALE = 64.0

def slot_numbers(expert_ids):
    blocks = expert_ids.reshape(N_EP, TOK_DEV * TOP)

    def per_device(block):
        marks = (block[:, None] == jnp.arange(EXPERTS, dtype=jnp.int32)[None, :]).astype(jnp.int32)
        before = jnp.cumsum(marks, axis=0) - marks
        return lax.optimization_barrier(jnp.sum(before * marks, axis=1)).astype(jnp.int32)
    return lax.map(per_device, blocks).reshape(TOKENS, TOP)

def expert_forward(packed):
    inputs, w_gate, w_up, w_down = packed
    gate_pre = jnp.dot(inputs, w_gate.T, preferred_element_type=jnp.float32)
    up_pre = jnp.dot(inputs, w_up.T, preferred_element_type=jnp.float32)
    sigma = jax.nn.sigmoid(gate_pre)
    active = (gate_pre * sigma * up_pre).astype(jnp.bfloat16)
    output = jnp.zeros((inputs.shape[0], D), jnp.float32)
    for group in range(FF // UNITS):
        start_col = group * UNITS
        part_sum = jnp.dot(active[:, start_col:start_col + UNITS], w_down[start_col:start_col + UNITS, :], preferred_element_type=jnp.float32).astype(jnp.bfloat16)
        output = output + lax.optimization_barrier(part_sum).astype(jnp.float32)
    return output

def expert_backward(packed):
    inputs, grads_in, w_gate, w_up, w_down = packed
    gate_pre = jnp.dot(inputs, w_gate.T, preferred_element_type=jnp.float32)
    up_pre = jnp.dot(inputs, w_up.T, preferred_element_type=jnp.float32)
    sigma = jax.nn.sigmoid(gate_pre)
    active = (gate_pre * sigma * up_pre).astype(jnp.bfloat16)
    d_active = jnp.dot(grads_in, w_down.T, preferred_element_type=jnp.float32)
    grad_down = jnp.dot(active.T, grads_in, preferred_element_type=jnp.float32).astype(jnp.bfloat16)
    d_gate = (d_active * up_pre * sigma * (1.0 + gate_pre * (1.0 - sigma))).astype(jnp.bfloat16)
    d_up = (d_active * gate_pre * sigma).astype(jnp.bfloat16)
    grad_gate = jnp.dot(d_gate.T, inputs, preferred_element_type=jnp.float32).astype(jnp.bfloat16)
    grad_up = jnp.dot(d_up.T, inputs, preferred_element_type=jnp.float32).astype(jnp.bfloat16)
    d_inputs = jnp.zeros((inputs.shape[0], D), jnp.float32)
    for group in range(FF // UNITS):
        start_col = group * UNITS
        part_sum = (jnp.dot(d_gate[:, start_col:start_col + UNITS], w_gate[start_col:start_col + UNITS, :], preferred_element_type=jnp.float32) + jnp.dot(d_up[:, start_col:start_col + UNITS], w_up[start_col:start_col + UNITS, :], preferred_element_type=jnp.float32)).astype(jnp.bfloat16)
        d_inputs = d_inputs + lax.optimization_barrier(part_sum).astype(jnp.float32)
    return (grad_gate, grad_up, grad_down, d_inputs)

def reference(hidden_in, norm_gain, expert_ids, routing_weight, labels, grad_later, head_weight, gate_weight, up_weight, down_weight):
    gate_three = gate_weight.reshape(EXPERTS, FF, D)
    up_three = up_weight.reshape(EXPERTS, FF, D)
    down_three = down_weight.reshape(EXPERTS, FF, D)
    hidden_wide = hidden_in.astype(jnp.float32)
    inv_rms = lax.rsqrt(lax.optimization_barrier(jnp.sum(hidden_wide * hidden_wide, axis=1, keepdims=True)) / D + EPS)
    normed = (hidden_wide * inv_rms * norm_gain[None, :]).astype(jnp.bfloat16)
    slots = slot_numbers(expert_ids)
    source = (jnp.arange(TOKENS, dtype=jnp.int32) // TOK_DEV).astype(jnp.int32)[:, None]
    rows_each = N_EP * CAP
    targets = (expert_ids * rows_each + source * CAP + slots).astype(jnp.int32)
    buffer = jnp.zeros((EXPERTS * rows_each, D), jnp.bfloat16)
    for slot_rank in range(TOP):
        buffer = buffer.at[targets[:, slot_rank]].set(normed)
    buffer = buffer.reshape(EXPERTS, rows_each, D)
    outputs = lax.map(expert_forward, (buffer, gate_three, up_three, down_three)).reshape(EXPERTS * rows_each, D)
    mixed = jnp.zeros((TOKENS, D), jnp.float32)
    for slot_rank in range(TOP):
        mixed = mixed + routing_weight[:, slot_rank:slot_rank + 1] * outputs[targets[:, slot_rank]]
    outcome = (hidden_wide + mixed).astype(jnp.bfloat16)
    logits = jnp.dot(outcome, head_weight, preferred_element_type=jnp.float32)
    classes = (labels[:, None] == jnp.arange(LABELS, dtype=jnp.int32)[None, :]).astype(jnp.float32)
    totals = lax.optimization_barrier(jnp.sum(jnp.exp(logits), axis=1, keepdims=True))
    token_loss = jnp.log(totals[:, 0]) - lax.optimization_barrier(jnp.sum(logits * classes, axis=1))
    d_logits = (jnp.exp(logits) / totals - classes) * LOSS_SCALE
    d_outcome = jnp.dot(d_logits, head_weight.astype(jnp.float32).T, precision=lax.Precision.HIGHEST) + grad_later.astype(jnp.float32)
    d_rounded = lax.optimization_barrier(d_outcome.astype(jnp.bfloat16)).astype(jnp.float32)
    grad_buffer = jnp.zeros((EXPERTS * rows_each, D), jnp.bfloat16)
    for slot_rank in range(TOP):
        scaled_rows = (routing_weight[:, slot_rank:slot_rank + 1] * d_rounded).astype(jnp.bfloat16)
        grad_buffer = grad_buffer.at[targets[:, slot_rank]].set(scaled_rows)
    grad_buffer = grad_buffer.reshape(EXPERTS, rows_each, D)
    grad_gate, grad_up, grad_down, d_inputs = lax.map(expert_backward, (buffer, grad_buffer, gate_three, up_three, down_three))
    d_inputs = d_inputs.reshape(EXPERTS * rows_each, D)
    d_normed = jnp.zeros((TOKENS, D), jnp.float32)
    for slot_rank in range(TOP):
        d_normed = d_normed + d_inputs[targets[:, slot_rank]]
    d_scaled = d_normed * norm_gain[None, :]
    slope = lax.optimization_barrier(jnp.sum(d_scaled * hidden_wide, axis=1, keepdims=True)) / D
    d_hidden = inv_rms * d_scaled - hidden_wide * (inv_rms * inv_rms * inv_rms) * slope
    grad_input = (d_outcome + d_hidden).astype(jnp.bfloat16)
    return (token_loss, outcome, grad_input, grad_gate.reshape(EXPERTS * FF, D), grad_up.reshape(EXPERTS * FF, D), grad_down.reshape(EXPERTS * FF, D))
```

```python
import functools

import jax
import jax.numpy as jnp
from jax import lax
from jax.experimental import pallas as pl
from jax.experimental.pallas import tpu as pltpu
from jax.sharding import PartitionSpec as P

FF = 768
EPS = 1e-06
LOSS_SCALE = 64.0
CAP = 12
LABELS = 4
QUAD = 4
LANES = 128
MESH = pl.DeviceIdType.MESH
F32 = jnp.float32
BF16 = jnp.bfloat16


def place(nj):
    ep = lax.axis_index("ep")
    t = lax.axis_index("tp")
    z = lax.div(ep, nj)
    j = lax.rem(ep, nj)
    return z, j, t


def z_order(nz):
    half = nz // 2
    order = []
    for back in range(half + 1):
        for k in (half - back, half + back):
            if 0 < k < nz and k not in order:
                order.append(k)
    return order


def rcopy(src, dst, send, recv, device):
    return pltpu.make_async_remote_copy(
        src_ref=src, dst_ref=dst, send_sem=send, recv_sem=recv, device_id=device, device_id_type=MESH
    )


def later(*args):
    return lambda: rcopy(*args)


def local_copy(*args):
    return lambda: pltpu.make_async_copy(*args)


def enter(nz, nj):
    z, j, t = place(nj)
    barrier = pltpu.get_barrier_semaphore()
    for k in range(1, nz):
        pl.semaphore_signal(
            barrier, inc=1, device_id={"ep": lax.rem(z + k, nz) * nj + j}, device_id_type=MESH
        )
    for k in range(1, nj):
        pl.semaphore_signal(
            barrier, inc=1, device_id={"ep": z * nj + lax.rem(j + k, nj)}, device_id_type=MESH
        )
    for k in range(1, 4):
        pl.semaphore_signal(barrier, inc=1, device_id={"tp": lax.rem(t + k, 4)}, device_id_type=MESH)
    pl.semaphore_wait(barrier, nz - 1 + nj - 1 + 3)


def column(t, f, chunks):
    return pl.ds(pl.multiple_of((t * chunks + f) * LANES, LANES), LANES)


def expert_keys(meta, z, ne):
    toks = meta.shape[1]
    names = (lax.broadcasted_iota(jnp.int32, (ne, toks), 0) + z * ne).astype(F32)
    named = jnp.zeros((ne, toks), F32)
    weight = jnp.zeros((ne, toks), F32)
    for k in range(8):
        hit = meta[k : k + 1, :] == names
        named = jnp.where(hit, 1.0, named)
        weight = jnp.where(hit, meta[8 + k : 9 + k, :], weight)
    earlier = (
        lax.broadcasted_iota(jnp.int32, (toks, toks), 0) < lax.broadcasted_iota(jnp.int32, (toks, toks), 1)
    ).astype(F32)
    rank = jnp.dot(named.astype(BF16), earlier.astype(BF16), preferred_element_type=F32)
    return jnp.where(named > 0.0, rank, -64.0), weight


def split(value):
    high = value.astype(BF16)
    return high, (value - high.astype(F32)).astype(BF16)


def build_pick(meta_ref, z, nz, ne, pick_hi, pick_lo):
    for zz in range(nz):
        q, zq = zz // QUAD, zz % QUAD
        key, weight = expert_keys(meta_ref[zz], z, ne)
        key = key + float(CAP * zq)
        row = lax.broadcasted_iota(jnp.int32, (ne, QUAD * CAP, LANES), 1).astype(F32)
        at = row == key[:, None, :]
        where = slice(zq * LANES, (zq + 1) * LANES)
        if pick_lo is None:
            one = jnp.where(at, 1.0, 0.0).astype(BF16)
            pick_hi[q, :, where] = one.reshape(ne * QUAD * CAP, LANES)
        else:
            high, low = split(jnp.where(at, weight[:, None, :], 0.0))
            pick_hi[q, :, where] = high.reshape(ne * QUAD * CAP, LANES)
            pick_lo[q, :, where] = low.reshape(ne * QUAD * CAP, LANES)


def build_place(meta_ref, z, nz, ne, place_hi, place_lo):
    wide = ne * QUAD * CAP
    expert = lax.broadcasted_iota(jnp.int32, (ne, wide), 0).astype(F32)
    lane = lax.broadcasted_iota(jnp.int32, (ne, wide), 1).astype(F32)
    start = expert * float(QUAD * CAP)
    spread = jnp.where((lane >= start) & (lane < start + float(QUAD * CAP)), 1.0, 0.0)
    base = jnp.sum(spread * start, axis=0, keepdims=True)
    within = lane[0:1] - base
    spread = spread.astype(BF16)
    for zz in range(nz):
        q, zq = zz // QUAD, zz % QUAD
        key, weight = expert_keys(meta_ref[zz], z, ne)
        key = key + float(CAP * zq)
        high, low = split(weight)
        fill = jnp.zeros((LANES - 3 * ne, LANES), F32)
        stack = jnp.concatenate([key, high.astype(F32), low.astype(F32), fill], axis=0)
        turned = jnp.transpose(stack).astype(BF16)
        keys = jnp.dot(turned[:, 0:ne], spread, preferred_element_type=F32)
        at = keys == within
        where = slice(zq * LANES, (zq + 1) * LANES)
        if place_lo is None:
            place_hi[q, where, :] = jnp.where(at, 1.0, 0.0).astype(BF16)
        else:
            highs = jnp.dot(turned[:, ne : 2 * ne], spread, preferred_element_type=F32)
            lows = jnp.dot(turned[:, 2 * ne : 3 * ne], spread, preferred_element_type=F32)
            place_hi[q, where, :] = jnp.where(at, highs, 0.0).astype(BF16)
            place_lo[q, where, :] = jnp.where(at, lows, 0.0).astype(BF16)


class Exchange:
    def __init__(self, nj, buf, send, recv):
        self.t = lax.axis_index("tp")
        self.buf, self.send, self.recv = buf, send, recv

    def copies(self):
        t = self.t
        for k in range(1, 4):
            to = lax.rem(t + k, 4)
            yield later(
                self.buf.at[t], self.buf.at[t], self.send.at[k], self.recv.at[t], {"tp": to}
            ), later(self.buf.at[t], self.buf.at[to], self.send.at[k], self.recv.at[to], {"tp": to})

    def start(self, value):
        self.buf[self.t] = value
        for out, _ in self.copies():
            out().start()

    def total(self):
        for _, arriving in self.copies():
            arriving().wait_recv()
        return (self.buf[0] + self.buf[1]) + (self.buf[2] + self.buf[3])

    def drain(self):
        for out, _ in self.copies():
            out().wait_send()


def to_row(col):
    return jnp.transpose(jnp.broadcast_to(col, (LANES, LANES)))[0:8, :]


def to_columns(row):
    return jnp.transpose(jnp.broadcast_to(row, (LANES, LANES)))


class Dispatch:
    def __init__(self, nz, nj, chunks, pick_hi, pick_lo, out, scratch):
        self.nz, self.nj, self.chunks = nz, nj, chunks
        self.z, self.j, self.t = place(nj)
        self.pick_hi, self.pick_lo, self.out = pick_hi, pick_lo, out
        (self.zbuf, self.xsend, self.xrecv, self.zss, self.zrs, self.xss, self.xrs, self.xl,
         self.yss, self.yrs, self.yl) = scratch

    @staticmethod
    def scratch(nz, nj, chunks):
        rows = nz * CAP
        return [
            pltpu.VMEM((chunks, nz, LANES, LANES), BF16),
            pltpu.VMEM((chunks, nj, 2, rows, LANES), BF16),
            pltpu.VMEM((chunks, 2, nj, rows, LANES), BF16),
            pltpu.SemaphoreType.DMA((chunks, nz)),
            pltpu.SemaphoreType.DMA((chunks, nz)),
            pltpu.SemaphoreType.DMA((chunks, nj)),
            pltpu.SemaphoreType.DMA((chunks, nj)),
            pltpu.SemaphoreType.DMA((chunks,)),
            pltpu.SemaphoreType.DMA((chunks, 3)),
            pltpu.SemaphoreType.DMA((chunks, 3)),
            pltpu.SemaphoreType.DMA((chunks,)),
        ]

    def z_copies(self, f):
        z, j, nz, nj = self.z, self.j, self.nz, self.nj
        for k in z_order(nz):
            to = lax.rem(z + k, nz)
            device = {"ep": to * nj + j}
            mine = self.zbuf.at[f, z]
            yield later(mine, mine, self.zss.at[f, k], self.zrs.at[f, z], device), later(
                mine, self.zbuf.at[f, to], self.zss.at[f, k], self.zrs.at[f, to], device
            )

    def z_send(self, f, value):
        self.zbuf[f, self.z] = value
        for out, _ in self.z_copies(f):
            out().start()

    def pick(self, f):
        for _, arriving in self.z_copies(f):
            arriving().wait_recv()
        nj, rows = self.nj, QUAD * CAP
        for q in range(self.nz // QUAD):
            block = self.zbuf[f, q * QUAD : (q + 1) * QUAD].reshape(QUAD * LANES, LANES)
            got = jnp.dot(self.pick_hi[q], block, preferred_element_type=F32)
            if self.pick_lo is not None:
                got = got + jnp.dot(self.pick_lo[q], block, preferred_element_type=F32)
            self.xsend[f, :, :, q * rows : (q + 1) * rows, :] = got.astype(BF16).reshape(nj, 2, rows, LANES)

    def x_copies(self, f):
        z, j, nj = self.z, self.j, self.nj
        for k in range(1, nj):
            to = lax.rem(j + k, nj)
            device = {"ep": z * nj + to}
            yield later(
                self.xsend.at[f, to], self.xrecv.at[f, :, j], self.xss.at[f, k], self.xrs.at[f, j], device
            ), later(
                self.xsend.at[f, to], self.xrecv.at[f, :, to], self.xss.at[f, k], self.xrs.at[f, to], device
            )

    def x_local(self, f):
        return local_copy(self.xsend.at[f, self.j], self.xrecv.at[f, :, self.j], self.xl.at[f])

    def x_send(self, f):
        for out, _ in self.x_copies(f):
            out().start()
        self.x_local(f)().start()

    def x_wait(self, f):
        for _, arriving in self.x_copies(f):
            arriving().wait_recv()
        self.x_local(f)().wait()

    def y_copies(self, f):
        t = self.t
        half = lax.div(t, 2)
        mate = t + 1 - 2 * lax.rem(t, 2)
        across = 3 - t
        mine, theirs = self.out.at[:, :, column(t, f, self.chunks)], self.out.at[:, :, column(across, f, self.chunks)]
        far = self.out.at[:, :, column(3 - mate, f, self.chunks)]
        near = self.out.at[:, :, column(mate, f, self.chunks)]
        src = self.xrecv.at[f, half]
        other = self.xrecv.at[f, 1 - half]
        sends = (
            later(src, mine, self.yss.at[f, 0], self.yrs.at[f, 0], {"tp": mate}),
            later(other, mine, self.yss.at[f, 1], self.yrs.at[f, 1], {"tp": across}),
            later(theirs, theirs, self.yss.at[f, 2], self.yrs.at[f, 2], {"tp": mate}),
        )
        arrivals = (
            later(src, near, self.yss.at[f, 0], self.yrs.at[f, 0], {"tp": mate}),
            later(src, theirs, self.yss.at[f, 1], self.yrs.at[f, 1], {"tp": across}),
            later(src, far, self.yss.at[f, 2], self.yrs.at[f, 2], {"tp": mate}),
        )
        return sends, arrivals, local_copy(src, mine, self.yl.at[f])

    def y_send(self, f):
        sends, _, local = self.y_copies(f)
        sends[1]().start()
        sends[0]().start()
        local().start()

    def y_forward(self, f):
        sends, arrivals, _ = self.y_copies(f)
        arrivals[1]().wait_recv()
        sends[2]().start()

    def run(self):
        n = self.chunks
        for step in range(n + 2):
            if step < n:
                self.pick(step)
                self.x_send(step)
            if 0 <= step - 1 < n:
                self.x_wait(step - 1)
                self.y_send(step - 1)
            if 0 <= step - 2 < n:
                self.y_forward(step - 2)
        for f in range(n):
            _, arrivals, local = self.y_copies(f)
            arrivals[0]().wait_recv()
            arrivals[2]().wait_recv()
            local().wait()

    def drain(self):
        for f in range(self.chunks):
            for out, _ in self.z_copies(f):
                out().wait_send()
            for out, _ in self.x_copies(f):
                out().wait_send()
            for out in self.y_copies(f)[0]:
                out().wait_send()


class Combine:
    def __init__(self, nz, nj, chunks, value, place_hi, place_lo, scratch):
        self.nz, self.nj, self.chunks, self.value = nz, nj, chunks, value
        self.z, self.j, self.t = place(nj)
        self.place_hi, self.place_lo = place_hi, place_lo
        (self.yr, self.ysum, self.xs, self.xr, self.zs, self.zr, self.yss, self.yrs,
         self.xss, self.xrs, self.xl, self.zss, self.zrs) = scratch

    @staticmethod
    def scratch(nz, nj, chunks):
        rows = nz * CAP
        return [
            pltpu.VMEM((chunks, 2, nj, rows, LANES), BF16),
            pltpu.VMEM((chunks, nj, rows, LANES), BF16),
            pltpu.VMEM((chunks, 2, nj, rows, LANES), BF16),
            pltpu.VMEM((chunks, nj, 2, rows, LANES), BF16),
            pltpu.VMEM((chunks, nz, LANES, LANES), BF16),
            pltpu.VMEM((chunks, nz, LANES, LANES), BF16),
            pltpu.SemaphoreType.DMA((chunks, 3)),
            pltpu.SemaphoreType.DMA((chunks, 3)),
            pltpu.SemaphoreType.DMA((chunks, nj)),
            pltpu.SemaphoreType.DMA((chunks, nj)),
            pltpu.SemaphoreType.DMA((chunks,)),
            pltpu.SemaphoreType.DMA((chunks, nz)),
            pltpu.SemaphoreType.DMA((chunks, nz)),
        ]

    def y_copies(self, f):
        t = self.t
        half = lax.div(t, 2)
        mate = t + 1 - 2 * lax.rem(t, 2)
        across = 3 - t
        sends = (
            later(self.value.at[:, :, column(mate, f, self.chunks)], self.yr.at[f, 0], self.yss.at[f, 0],
                  self.yrs.at[f, 0], {"tp": mate}),
            later(self.value.at[:, :, column(3 - mate, f, self.chunks)], self.yr.at[f, 1], self.yss.at[f, 1],
                  self.yrs.at[f, 1], {"tp": mate}),
            later(self.ysum.at[f], self.xs.at[f, half], self.yss.at[f, 2], self.yrs.at[f, 2],
                  {"tp": across}),
        )
        last = later(self.ysum.at[f], self.xs.at[f, 1 - half], self.yss.at[f, 2], self.yrs.at[f, 2],
                     {"tp": across})
        return sends, (sends[0], sends[1], last)

    def start(self):
        for f in range(self.chunks):
            sends, _ = self.y_copies(f)
            sends[1]().start()
            sends[0]().start()

    def y_sum(self, f):
        t = self.t
        sends, arrivals = self.y_copies(f)
        arrivals[1]().wait_recv()
        for i in range(self.nj):
            own = self.value[i, :, column(3 - t, f, self.chunks)].astype(F32)
            self.ysum[f, i] = (own + self.yr[f, 1, i].astype(F32)).astype(BF16)
        sends[2]().start()
        arrivals[0]().wait_recv()
        half = lax.div(t, 2)
        for i in range(self.nj):
            own = self.value[i, :, column(t, f, self.chunks)].astype(F32)
            self.xs[f, half, i] = (own + self.yr[f, 0, i].astype(F32)).astype(BF16)

    def x_copies(self, f):
        z, j, nj = self.z, self.j, self.nj
        for k in range(1, nj):
            to = lax.rem(j + k, nj)
            device = {"ep": z * nj + to}
            yield later(
                self.xs.at[f, :, to], self.xr.at[f, j], self.xss.at[f, k], self.xrs.at[f, j], device
            ), later(
                self.xs.at[f, :, to], self.xr.at[f, to], self.xss.at[f, k], self.xrs.at[f, to], device
            )

    def x_local(self, f):
        return local_copy(self.xs.at[f, :, self.j], self.xr.at[f, self.j], self.xl.at[f])

    def x_send(self, f):
        self.y_copies(f)[1][2]().wait_recv()
        for out, _ in self.x_copies(f):
            out().start()
        self.x_local(f)().start()

    def z_copies(self, f):
        z, j, nz, nj = self.z, self.j, self.nz, self.nj
        for k in z_order(nz):
            to = lax.rem(z + k, nz)
            device = {"ep": to * nj + j}
            yield later(
                self.zs.at[f, to], self.zr.at[f, z], self.zss.at[f, k], self.zrs.at[f, z], device
            ), later(
                self.zs.at[f, to], self.zr.at[f, to], self.zss.at[f, k], self.zrs.at[f, to], device
            )

    def mix(self, f):
        for _, arriving in self.x_copies(f):
            arriving().wait_recv()
        self.x_local(f)().wait()
        rows = QUAD * CAP
        for q in range(self.nz // QUAD):
            got = self.xr[f, :, :, q * rows : (q + 1) * rows, :].reshape(self.nj * 2 * rows, LANES)
            part = jnp.dot(self.place_hi[q], got, preferred_element_type=F32)
            if self.place_lo is not None:
                part = part + jnp.dot(self.place_lo[q], got, preferred_element_type=F32)
            self.zs[f, q * QUAD : (q + 1) * QUAD] = part.astype(BF16).reshape(QUAD, LANES, LANES)
        for out, _ in self.z_copies(f):
            out().start()

    def run(self):
        n = self.chunks
        for step in range(n + 2):
            if step < n:
                self.y_sum(step)
            if 0 <= step - 1 < n:
                self.x_send(step - 1)
            if 0 <= step - 2 < n:
                self.mix(step - 2)

    def result(self, f):
        for _, arriving in self.z_copies(f):
            arriving().wait_recv()
        total = self.zs[f, self.z].astype(F32)
        for k in range(1, self.nz):
            total = total + self.zr[f, lax.rem(self.z + k, self.nz)].astype(F32)
        return total

    def drain(self):
        for f in range(self.chunks):
            for out in self.y_copies(f)[0]:
                out().wait_send()
            for out, _ in self.x_copies(f):
                out().wait_send()
            for out, _ in self.z_copies(f):
                out().wait_send()


def lanes(f):
    return slice(f * LANES, (f + 1) * LANES)


def first_kernel(nz, nj, chunks, hidden_ref, gain_ref, own_ref, out_ref, meta_ref, inv_ref,
                 pick_ref, sum_buf, sum_ss, sum_rs, meta_ss, meta_rs, *scratch):
    z, j, t = place(nj)
    enter(nz, nj)
    squares = Exchange(nj, sum_buf, sum_ss, sum_rs)
    wide = hidden_ref[...].astype(F32)
    squares.start(to_row(jnp.sum(wide * wide, axis=1, keepdims=True)))

    def meta_copies():
        for k in range(1, nz):
            to = lax.rem(z + k, nz)
            device = {"ep": to * nj + j}
            yield later(own_ref, meta_ref.at[z], meta_ss.at[k], meta_rs.at[z], device), later(
                own_ref, meta_ref.at[to], meta_ss.at[k], meta_rs.at[to], device
            )

    for out, _ in meta_copies():
        out().start()
    meta_ref[z] = own_ref[...]
    move = Dispatch(nz, nj, chunks, pick_ref, None, out_ref, scratch)
    total = to_columns(squares.total()[0:1, :])
    inv = lax.rsqrt(total / (4 * chunks * LANES) + EPS)
    inv_ref[...] = inv
    for f in range(chunks):
        normed = hidden_ref[:, lanes(f)].astype(F32) * inv * gain_ref[0:1, lanes(f)]
        move.z_send(f, normed.astype(BF16))
    for _, arriving in meta_copies():
        arriving().wait_recv()
    build_pick(meta_ref, z, nz, 2 * nj, pick_ref, None)
    move.run()
    move.drain()
    squares.drain()
    for out, _ in meta_copies():
        out().wait_send()


def middle_kernel(nz, nj, chunks, value_ref, meta_ref, hidden_ref, later_ref, head_ref, labels_ref,
                  outcome_ref, loss_ref, dout_ref, grads_ref,
                  place_hi, place_lo, pick_hi, pick_lo, sum_buf, sum_ss, sum_rs, *scratch):
    z, j, t = place(nj)
    enter(nz, nj)
    cut = len(Combine.scratch(nz, nj, chunks))
    back = Combine(nz, nj, chunks, value_ref, place_hi, place_lo, scratch[:cut])
    back.start()
    build_place(meta_ref, z, nz, 2 * nj, place_hi, place_lo)
    build_pick(meta_ref, z, nz, 2 * nj, pick_hi, pick_lo)
    back.run()
    logits = jnp.zeros((8, LANES), F32)
    for f in range(chunks):
        mixed = back.result(f)
        outcome = (hidden_ref[:, lanes(f)].astype(F32) + mixed).astype(BF16)
        outcome_ref[:, lanes(f)] = outcome
        logits = logits + lax.dot_general(
            head_ref[:, lanes(f)], outcome, (((1,), (1,)), ((), ())), preferred_element_type=F32
        )
    sums = Exchange(nj, sum_buf, sum_ss, sum_rs)
    sums.start(logits)
    logits = sums.total()
    row = lax.broadcasted_iota(jnp.int32, (8, LANES), 0)
    live = row < LABELS
    hot = jnp.where(row == labels_ref[0:1, :], 1.0, 0.0)
    powers = jnp.where(live, jnp.exp(jnp.where(live, logits, 0.0)), 0.0)
    totals = jnp.sum(powers, axis=0, keepdims=True)
    loss = jnp.log(totals) - jnp.sum(logits * hot, axis=0, keepdims=True)
    loss_ref[...] = jnp.broadcast_to(loss, (8, LANES))
    d_logits = (powers / totals - hot) * LOSS_SCALE
    d_logits = jnp.concatenate([d_logits, jnp.zeros((LANES - 8, LANES), F32)], axis=0)
    d_logits = jnp.transpose(d_logits)
    move = Dispatch(nz, nj, chunks, pick_hi, pick_lo, grads_ref, scratch[cut:])
    for f in range(chunks):
        d_outcome = later_ref[:, lanes(f)].astype(F32)
        term = jnp.zeros((LANES, LANES), F32)
        for label in range(LABELS):
            weight = head_ref[label : label + 1, lanes(f)].astype(F32)
            term = term + d_logits[:, label : label + 1] * weight
        d_outcome = term + d_outcome
        dout_ref[:, lanes(f)] = d_outcome
        move.z_send(f, d_outcome.astype(BF16))
    move.run()
    move.drain()
    sums.drain()
    back.drain()


def last_kernel(nz, nj, chunks, value_ref, meta_ref, hidden_ref, gain_ref, inv_ref, dout_ref,
                grad_ref, place_ref, scaled_ref, sum_buf, sum_ss, sum_rs, *scratch):
    z, j, t = place(nj)
    enter(nz, nj)
    back = Combine(nz, nj, chunks, value_ref, place_ref, None, scratch)
    back.start()
    build_place(meta_ref, z, nz, 2 * nj, place_ref, None)
    back.run()
    slope = jnp.zeros((LANES, LANES), F32)
    for f in range(chunks):
        scaled = back.result(f) * gain_ref[0:1, lanes(f)]
        scaled_ref[:, lanes(f)] = scaled
        slope = slope + scaled * hidden_ref[:, lanes(f)].astype(F32)
    sums = Exchange(nj, sum_buf, sum_ss, sum_rs)
    sums.start(to_row(jnp.sum(slope, axis=1, keepdims=True)))
    slope = to_columns(sums.total()[0:1, :]) / (4 * chunks * LANES)
    inv = inv_ref[...]
    cube = inv * inv * inv
    for f in range(chunks):
        d_hidden = inv * scaled_ref[:, lanes(f)] - hidden_ref[:, lanes(f)].astype(F32) * cube * slope
        grad_ref[:, lanes(f)] = (dout_ref[:, lanes(f)] + d_hidden).astype(BF16)
    sums.drain()
    back.drain()


def shards(nz, nj, hidden_in, norm_gain, expert_ids, routing_weight, labels, grad_later, head_weight,
           gate_weight, up_weight, down_weight):
    width = gate_weight.shape[1]
    chunks = hidden_in.shape[1] // LANES
    ne = 2 * nj
    nq = nz // QUAD
    rows = nz * CAP
    high = ne * QUAD * CAP
    tall = QUAD * LANES
    vmem = pl.BlockSpec(memory_space=pltpu.VMEM)
    sems = [pltpu.SemaphoreType.DMA((4,)), pltpu.SemaphoreType.DMA((4,))]
    sums = [pltpu.VMEM((4, 8, LANES), F32)] + sems

    def call(kernel, name, ident, outs, scratch, *args):
        return pl.pallas_call(
            functools.partial(kernel, nz, nj, chunks),
            out_shape=outs,
            in_specs=[vmem] * len(args),
            out_specs=[vmem] * len(outs),
            scratch_shapes=scratch,
            name=name,
            compiler_params=pltpu.CompilerParams(collective_id=ident, has_side_effects=True),
        )(*args)

    buffer = jax.ShapeDtypeStruct((nj, rows, width), BF16)
    own = jnp.concatenate([expert_ids.T.astype(F32), routing_weight.T], axis=0)
    gain = norm_gain[None, :]
    head = jnp.concatenate([head_weight.T, jnp.zeros_like(head_weight.T)], axis=0)
    received, meta, inv = call(
        first_kernel, "dispatch_tokens", 1,
        [buffer, jax.ShapeDtypeStruct((nz, 16, LANES), F32), jax.ShapeDtypeStruct((LANES, LANES), F32)],
        [pltpu.VMEM((nq, high, tall), BF16)] + sums
        + [pltpu.SemaphoreType.DMA((nz,)), pltpu.SemaphoreType.DMA((nz,))]
        + Dispatch.scratch(nz, nj, chunks),
        hidden_in, gain, own,
    )
    received = received.reshape(nj * rows, width)

    def dot(a, b, ca, cb):
        return lax.dot_general(a, b, (((ca,), (cb,)), ((), ())), preferred_element_type=F32)

    gate_pre = dot(received, gate_weight, 1, 1)
    up_pre = dot(received, up_weight, 1, 1)
    sigma = jax.nn.sigmoid(gate_pre)
    active = (gate_pre * sigma * up_pre).astype(BF16)
    partial_value = dot(active, down_weight, 1, 0).astype(BF16)
    outcome, loss, d_outcome, grads_in = call(
        middle_kernel, "combine_head_dispatch", 2,
        [
            jax.ShapeDtypeStruct(hidden_in.shape, BF16),
            jax.ShapeDtypeStruct((8, LANES), F32),
            jax.ShapeDtypeStruct(hidden_in.shape, F32),
            buffer,
        ],
        [pltpu.VMEM((nq, tall, high), BF16)] * 2 + [pltpu.VMEM((nq, high, tall), BF16)] * 2 + sums
        + Combine.scratch(nz, nj, chunks) + Dispatch.scratch(nz, nj, chunks),
        partial_value.reshape(nj, rows, width), meta, hidden_in, grad_later, head, labels[None, :],
    )
    grads_in = grads_in.reshape(nj * rows, width)
    d_active = dot(grads_in, down_weight, 1, 1)
    d_gate = (d_active * up_pre * sigma * (1.0 + gate_pre * (1.0 - sigma))).astype(BF16)
    d_up = (d_active * gate_pre * sigma).astype(BF16)
    d_partial = (dot(d_gate, gate_weight, 1, 0) + dot(d_up, up_weight, 1, 0)).astype(BF16)
    grad_down = dot(active, grads_in, 0, 0).astype(BF16)
    grad_gate = dot(d_gate, received, 0, 0).astype(BF16)
    grad_up = dot(d_up, received, 0, 0).astype(BF16)
    (grad_input,) = call(
        last_kernel, "combine_grad", 3,
        [jax.ShapeDtypeStruct(hidden_in.shape, BF16)],
        [pltpu.VMEM((nq, tall, high), BF16), pltpu.VMEM(hidden_in.shape, F32)] + sums
        + Combine.scratch(nz, nj, chunks),
        d_partial.reshape(nj, rows, width), meta, hidden_in, gain, inv, d_outcome,
    )
    return loss[0], outcome, grad_input, grad_gate, grad_up, grad_down


def solution(mesh, nj=8):
    nz = mesh.shape["ep"] // nj
    in_specs = (
        P("ep", "tp"),
        P("tp"),
        P("ep", None),
        P("ep", None),
        P("ep"),
        P("ep", "tp"),
        P("tp", None),
        P(("ep", "tp"), None),
        P(("ep", "tp"), None),
        P(("ep", "tp"), None),
    )
    out_specs = (
        P("ep"),
        P("ep", "tp"),
        P("ep", "tp"),
        P(("ep", "tp"), None),
        P(("ep", "tp"), None),
        P(("ep", "tp"), None),
    )
    return jax.shard_map(
        functools.partial(shards, nz, nj), mesh=mesh, in_specs=in_specs, out_specs=out_specs, check_vma=False
    )
```

```python
import functools

import jax
import jax.numpy as jnp
from jax import lax
from jax.experimental import pallas as pl
from jax.experimental.pallas import tpu as pltpu
from jax.sharding import PartitionSpec as P

FF = 768
EPS = 1e-06
LOSS_SCALE = 64.0
CAP = 12
LABELS = 4
QUAD = 4
LANES = 128
MESH = pl.DeviceIdType.MESH
F32 = jnp.float32
BF16 = jnp.bfloat16


def place(nj):
    ep = lax.axis_index("ep")
    t = lax.axis_index("tp")
    z = lax.div(ep, nj)
    j = lax.rem(ep, nj)
    return z, j, t


def z_order(nz):
    half = nz // 2
    order = []
    for back in range(half + 1):
        for k in (half - back, half + back):
            if 0 < k < nz and k not in order:
                order.append(k)
    return order


def rcopy(src, dst, send, recv, device):
    return pltpu.make_async_remote_copy(
        src_ref=src, dst_ref=dst, send_sem=send, recv_sem=recv, device_id=device, device_id_type=MESH
    )


def later(*args):
    return lambda: rcopy(*args)


def local_copy(*args):
    return lambda: pltpu.make_async_copy(*args)


def enter(nz, nj):
    z, j, t = place(nj)
    barrier = pltpu.get_barrier_semaphore()
    for k in range(1, nz):
        pl.semaphore_signal(
            barrier, inc=1, device_id={"ep": lax.rem(z + k, nz) * nj + j}, device_id_type=MESH
        )
    for k in range(1, nj):
        pl.semaphore_signal(
            barrier, inc=1, device_id={"ep": z * nj + lax.rem(j + k, nj)}, device_id_type=MESH
        )
    for k in range(1, 4):
        pl.semaphore_signal(barrier, inc=1, device_id={"tp": lax.rem(t + k, 4)}, device_id_type=MESH)
    pl.semaphore_wait(barrier, nz - 1 + nj - 1 + 3)


def column(t, f, chunks):
    return pl.ds(pl.multiple_of((t * chunks + f) * LANES, LANES), LANES)


def expert_keys(meta, z, ne):
    toks = meta.shape[1]
    names = (lax.broadcasted_iota(jnp.int32, (ne, toks), 0) + z * ne).astype(F32)
    named = jnp.zeros((ne, toks), F32)
    weight = jnp.zeros((ne, toks), F32)
    for k in range(8):
        hit = meta[k : k + 1, :] == names
        named = jnp.where(hit, 1.0, named)
        weight = jnp.where(hit, meta[8 + k : 9 + k, :], weight)
    earlier = (
        lax.broadcasted_iota(jnp.int32, (toks, toks), 0) < lax.broadcasted_iota(jnp.int32, (toks, toks), 1)
    ).astype(F32)
    rank = jnp.dot(named.astype(BF16), earlier.astype(BF16), preferred_element_type=F32)
    return jnp.where(named > 0.0, rank, -64.0), weight


def split(value, parts):
    out = []
    for _ in range(parts):
        out.append(value.astype(BF16))
        value = value - out[-1].astype(F32)
    return out


def build_pick(meta_ref, z, nz, ne, pick, weights):
    rows = QUAD * CAP
    row = lax.broadcasted_iota(jnp.int32, (ne, rows, LANES), 1).astype(F32)
    lane = lax.broadcasted_iota(jnp.int32, (ne * rows, LANES), 1)
    for q in range(nz // QUAD):

        def one(zq, held):
            key, weight = expert_keys(meta_ref[q * QUAD + zq], z, ne)
            key = key + (CAP * zq).astype(F32)
            at = row == key[:, None, :]
            hot = jnp.where(at, 1.0, 0.0).astype(BF16).reshape(ne * rows, LANES)
            pick[q, :, pl.ds(pl.multiple_of(zq * LANES, LANES), LANES)] = hot
            share = jnp.where(at, weight[:, None, :], 0.0).reshape(ne * rows, LANES)
            return held + jnp.sum(share, axis=1, keepdims=True)

        held = lax.fori_loop(0, QUAD, one, jnp.zeros((ne * rows, 1), F32))
        held = jnp.broadcast_to(held, (ne * rows, LANES))
        high, middle, low = [part.astype(F32) for part in split(held, 3)]
        value = jnp.where(lane == 12, high, jnp.where(lane == 13, middle, jnp.where(lane == 14, low, 0.0)))
        weights[q] = value.astype(BF16)


def build_place(meta_ref, z, nz, ne, place_hi, place_lo, place_one):
    wide = ne * QUAD * CAP
    expert = lax.broadcasted_iota(jnp.int32, (ne, wide), 0).astype(F32)
    lane = lax.broadcasted_iota(jnp.int32, (ne, wide), 1).astype(F32)
    start = expert * float(QUAD * CAP)
    spread = jnp.where((lane >= start) & (lane < start + float(QUAD * CAP)), 1.0, 0.0)
    base = jnp.sum(spread * start, axis=0, keepdims=True)
    within = lane[0:1] - base
    spread = spread.astype(BF16)
    fill = jnp.zeros((LANES - 3 * ne, LANES), F32)

    for q in range(nz // QUAD):

        def one(zq, carry):
            key, weight = expert_keys(meta_ref[q * QUAD + zq], z, ne)
            key = key + (CAP * zq).astype(F32)
            high, low = split(weight, 2)
            stack = jnp.concatenate([key, high.astype(F32), low.astype(F32), fill], axis=0)
            turned = jnp.transpose(stack).astype(BF16)
            at = jnp.dot(turned[:, 0:ne], spread, preferred_element_type=F32) == within
            where = pl.ds(pl.multiple_of(zq * LANES, LANES), LANES)
            highs = jnp.dot(turned[:, ne : 2 * ne], spread, preferred_element_type=F32)
            lows = jnp.dot(turned[:, 2 * ne : 3 * ne], spread, preferred_element_type=F32)
            place_hi[q, where, :] = jnp.where(at, highs, 0.0).astype(BF16)
            place_lo[q, where, :] = jnp.where(at, lows, 0.0).astype(BF16)
            place_one[q, where, :] = jnp.where(at, 1.0, 0.0).astype(BF16)
            return carry

        lax.fori_loop(0, QUAD, one, 0)


class Exchange:
    def __init__(self, buf, send, recv):
        self.t = lax.axis_index("tp")
        self.buf, self.send, self.recv = buf, send, recv

    def copies(self):
        t = self.t
        for k in range(1, 4):
            to = lax.rem(t + k, 4)
            yield later(
                self.buf.at[t], self.buf.at[t], self.send.at[k], self.recv.at[t], {"tp": to}
            ), later(self.buf.at[t], self.buf.at[to], self.send.at[k], self.recv.at[to], {"tp": to})

    def start(self, value):
        self.buf[self.t] = value
        for out, _ in self.copies():
            out().start()

    def total(self):
        for _, arriving in self.copies():
            arriving().wait_recv()
        return (self.buf[0] + self.buf[1]) + (self.buf[2] + self.buf[3])

    def total_again(self):
        return (self.buf[0] + self.buf[1]) + (self.buf[2] + self.buf[3])

    def drain(self):
        for out, _ in self.copies():
            out().wait_send()


def to_row(col):
    return jnp.transpose(jnp.broadcast_to(col, (LANES, LANES)))[0:8, :]


def to_columns(row):
    return jnp.transpose(jnp.broadcast_to(row, (LANES, LANES)))


DMA = pltpu.SemaphoreType.DMA


def lanes(f):
    return slice(f * LANES, (f + 1) * LANES)


class Refs:
    def __init__(self, names, refs):
        for name, ref in zip(names, refs):
            setattr(self, name, ref)


class Along:
    def __init__(self, count, axis, nj, send, recv):
        self.z, self.j, _ = place(nj)
        self.count, self.axis, self.nj, self.send, self.recv = count, axis, nj, send, recv

    def each(self):
        for k in z_order(self.count):
            if self.axis == "z":
                to = lax.rem(self.z + k, self.count)
                yield k, to, {"ep": to * self.nj + self.j}
            else:
                to = lax.rem(self.j + k, self.count)
                yield k, to, {"ep": self.z * self.nj + to}

    def copies(self, f, source, landing):
        me = self.z if self.axis == "z" else self.j
        for k, to, device in self.each():
            yield (
                later(source(to), landing(me), self.send.at[f, k], self.recv.at[f, me], device),
                later(source(to), landing(to), self.send.at[f, k], self.recv.at[f, to], device),
            )


class Dispatch:
    names = ["zbuf", "xsend", "xrecv", "zss", "zrs", "xss", "xrs", "xl"]

    @staticmethod
    def scratch(nz, nj, chunks):
        rows = nz * CAP
        return [
            pltpu.VMEM((chunks, nz, LANES, LANES), BF16),
            pltpu.VMEM((chunks, nj, 2, rows, LANES), BF16),
            pltpu.VMEM((chunks, 2, nj, rows, LANES), BF16),
            DMA((chunks, nz)),
            DMA((chunks, nz)),
            DMA((chunks, nj)),
            DMA((chunks, nj)),
            DMA((chunks,)),
        ]

    def __init__(self, nz, nj, chunks, pick, added, half, refs):
        self.nz, self.nj, self.chunks, self.pick_ref, self.added, self.half = nz, nj, chunks, pick, added, half
        self.z, self.j, self.t = place(nj)
        r = self.r = Refs(self.names, refs)
        self.along_z = Along(nz, "z", nj, r.zss, r.zrs)
        self.along_x = Along(nj, "x", nj, r.xss, r.xrs)

    def z_copies(self, f):
        return self.along_z.copies(f, lambda to: self.r.zbuf.at[f, self.z], lambda z: self.r.zbuf.at[f, z])

    def z_send(self, f, value):
        self.r.zbuf[f, self.z] = value
        for out, _ in self.z_copies(f):
            out().start()

    def pick(self, f):
        for _, arriving in self.z_copies(f):
            arriving().wait_recv()
        nj, rows = self.nj, QUAD * CAP
        for q in range(self.nz // QUAD):
            block = self.r.zbuf[f, q * QUAD : (q + 1) * QUAD].reshape(QUAD * LANES, LANES)
            got = jnp.dot(self.pick_ref[q], block, preferred_element_type=F32).astype(BF16)
            if self.added is not None:
                got = got + self.added[q]
            self.r.xsend[f, :, :, q * rows : (q + 1) * rows, :] = got.reshape(nj, 2, rows, LANES)
        for out, _ in self.x_copies(f):
            out().start()
        self.x_local(f)().start()

    def x_copies(self, f):
        r, half = self.r, self.half
        if half is None:
            return self.along_x.copies(f, lambda to: r.xsend.at[f, to], lambda j: r.xrecv.at[f, :, j])
        return self.along_x.copies(f, lambda to: r.xsend.at[f, to, half], lambda j: r.xrecv.at[f, half, j])

    def x_local(self, f):
        r, j, half = self.r, self.j, self.half
        if half is None:
            return local_copy(r.xsend.at[f, j], r.xrecv.at[f, :, j], r.xl.at[f])
        return local_copy(r.xsend.at[f, j, half], r.xrecv.at[f, half, j], r.xl.at[f])

    def x_wait(self, f):
        for _, arriving in self.x_copies(f):
            arriving().wait_recv()
        self.x_local(f)().wait()

    def drain(self):
        for f in range(self.chunks):
            for out, _ in self.z_copies(f):
                out().wait_send()
            for out, _ in self.x_copies(f):
                out().wait_send()


class Gather:
    names = ["yss", "yrs", "yl"]

    @staticmethod
    def scratch(chunks):
        return [DMA((chunks, 3)), DMA((chunks, 3)), DMA((chunks,))]

    def __init__(self, chunks, source, out, refs):
        self.chunks, self.source, self.out = chunks, source, out
        self.t = lax.axis_index("tp")
        self.r = Refs(self.names, refs)

    def copies(self, f):
        t, r, out = self.t, self.r, self.out
        half = lax.div(t, 2)
        mate = t + 1 - 2 * lax.rem(t, 2)
        across = 3 - t
        mine, theirs = out.at[:, :, column(t, f, self.chunks)], out.at[:, :, column(across, f, self.chunks)]
        far = out.at[:, :, column(3 - mate, f, self.chunks)]
        near = out.at[:, :, column(mate, f, self.chunks)]
        src, other = self.source.at[f, half], self.source.at[f, 1 - half]
        sends = (
            later(src, mine, r.yss.at[f, 0], r.yrs.at[f, 0], {"tp": mate}),
            later(other, mine, r.yss.at[f, 1], r.yrs.at[f, 1], {"tp": across}),
            later(theirs, theirs, r.yss.at[f, 2], r.yrs.at[f, 2], {"tp": mate}),
        )
        arrivals = (
            later(src, near, r.yss.at[f, 0], r.yrs.at[f, 0], {"tp": mate}),
            later(src, theirs, r.yss.at[f, 1], r.yrs.at[f, 1], {"tp": across}),
            later(src, far, r.yss.at[f, 2], r.yrs.at[f, 2], {"tp": mate}),
        )
        return sends, arrivals, local_copy(src, mine, r.yl.at[f])

    def send(self, f):
        sends, _, local = self.copies(f)
        sends[1]().start()
        sends[0]().start()
        local().start()

    def forward(self, f):
        sends, arrivals, _ = self.copies(f)
        arrivals[1]().wait_recv()
        sends[2]().start()

    def wait(self, f):
        _, arrivals, local = self.copies(f)
        arrivals[0]().wait_recv()
        arrivals[2]().wait_recv()
        local().wait()

    def chunk(self, f):
        rows = self.out.shape[0] * self.out.shape[1]
        parts = [self.out[:, :, wide(s, f, self.chunks)].reshape(rows, LANES) for s in range(4)]
        return jnp.concatenate(parts, axis=1)

    def relayed(self, f):
        self.copies(f)[0][2]().wait_send()

    def drain(self):
        for f in range(self.chunks):
            for out in self.copies(f)[0][:2]:
                out().wait_send()


def wide(s, f, chunks):
    return slice((s * chunks + f) * LANES, (s * chunks + f + 1) * LANES)


def weight_chunk(ref, f, chunks):
    return jnp.concatenate([ref[:, wide(s, f, chunks)] for s in range(4)], axis=1)


class Combine:
    names = ["yr", "ysum", "xs", "xr", "zs", "zr", "yss", "yrs", "xss", "xrs", "xl", "zss", "zrs"]

    @staticmethod
    def scratch(nz, nj, chunks):
        rows = nz * CAP
        return [
            pltpu.VMEM((chunks, 2, nj, rows, LANES), BF16),
            pltpu.VMEM((chunks, nj, rows, LANES), BF16),
            pltpu.VMEM((chunks, 2, nj, rows, LANES), BF16),
            pltpu.VMEM((chunks, nj, 2, rows, LANES), BF16),
            pltpu.VMEM((chunks, nz, LANES, LANES), BF16),
            pltpu.VMEM((chunks, nz, LANES, LANES), BF16),
            DMA((chunks, 3)),
            DMA((chunks, 3)),
            DMA((chunks, nj)),
            DMA((chunks, nj)),
            DMA((chunks,)),
            DMA((chunks, nz)),
            DMA((chunks, nz)),
        ]

    def __init__(self, nz, nj, chunks, value, places, refs):
        self.nz, self.nj, self.chunks, self.value, self.places = nz, nj, chunks, value, places
        self.z, self.j, self.t = place(nj)
        r = self.r = Refs(self.names, refs)
        self.along_z = Along(nz, "z", nj, r.zss, r.zrs)
        self.along_x = Along(nj, "x", nj, r.xss, r.xrs)

    def y_copies(self, f):
        t, r, n = self.t, self.r, self.chunks
        half = lax.div(t, 2)
        mate = t + 1 - 2 * lax.rem(t, 2)
        across = 3 - t
        sends = (
            later(self.value.at[:, :, column(mate, f, n)], r.yr.at[f, 0], r.yss.at[f, 0], r.yrs.at[f, 0],
                  {"tp": mate}),
            later(self.value.at[:, :, column(3 - mate, f, n)], r.yr.at[f, 1], r.yss.at[f, 1], r.yrs.at[f, 1],
                  {"tp": mate}),
            later(r.ysum.at[f], r.xs.at[f, half], r.yss.at[f, 2], r.yrs.at[f, 2], {"tp": across}),
        )
        last = later(r.ysum.at[f], r.xs.at[f, 1 - half], r.yss.at[f, 2], r.yrs.at[f, 2], {"tp": across})
        return sends, (sends[0], sends[1], last)

    def put(self, f, value):
        for s in range(4):
            part = value[:, lanes(s)].reshape(self.value.shape[0], self.value.shape[1], LANES)
            self.value[:, :, wide(s, f, self.chunks)] = part
        sends, _ = self.y_copies(f)
        sends[1]().start()
        sends[0]().start()

    def sent(self):
        for f in range(self.chunks):
            sends, _ = self.y_copies(f)
            sends[1]().wait_send()
            sends[0]().wait_send()

    def y_sum(self, f):
        t, r, n = self.t, self.r, self.chunks
        sends, arrivals = self.y_copies(f)
        arrivals[1]().wait_recv()

        def far(i, carry):
            own = self.value[i, :, column(3 - t, f, n)].astype(F32)
            r.ysum[f, i] = (own + r.yr[f, 1, i].astype(F32)).astype(BF16)
            return carry

        lax.fori_loop(0, self.nj, far, 0)
        sends[2]().start()
        arrivals[0]().wait_recv()
        half = lax.div(t, 2)

        def near(i, carry):
            own = self.value[i, :, column(t, f, n)].astype(F32)
            r.xs[f, half, i] = (own + r.yr[f, 0, i].astype(F32)).astype(BF16)
            return carry

        lax.fori_loop(0, self.nj, near, 0)

    def x_copies(self, f):
        return self.along_x.copies(f, lambda to: self.r.xs.at[f, :, to], lambda j: self.r.xr.at[f, j])

    def x_local(self, f):
        return local_copy(self.r.xs.at[f, :, self.j], self.r.xr.at[f, self.j], self.r.xl.at[f])

    def x_send(self, f):
        self.y_copies(f)[1][2]().wait_recv()
        for out, _ in self.x_copies(f):
            out().start()
        self.x_local(f)().start()

    def z_copies(self, f):
        return self.along_z.copies(f, lambda to: self.r.zs.at[f, to], lambda z: self.r.zr.at[f, z])

    def mix(self, f):
        for _, arriving in self.x_copies(f):
            arriving().wait_recv()
        self.x_local(f)().wait()
        rows = QUAD * CAP
        for q in range(self.nz // QUAD):
            got = self.r.xr[f, :, :, q * rows : (q + 1) * rows, :].reshape(self.nj * 2 * rows, LANES)
            part = jnp.dot(self.places[0][q], got, preferred_element_type=F32)
            for more in self.places[1:]:
                part = part + jnp.dot(more[q], got, preferred_element_type=F32)
            self.r.zs[f, q * QUAD : (q + 1) * QUAD] = part.astype(BF16).reshape(QUAD, LANES, LANES)
        for out, _ in self.z_copies(f):
            out().start()

    def result(self, f):
        for _, arriving in self.z_copies(f):
            arriving().wait_recv()
        total = self.r.zs[f, self.z].astype(F32)
        for k in range(1, self.nz):
            total = total + self.r.zr[f, lax.rem(self.z + k, self.nz)].astype(F32)
        return total

    def drain(self):
        for f in range(self.chunks):
            self.y_copies(f)[0][2]().wait_send()
            for out, _ in self.x_copies(f):
                out().wait_send()
            for out, _ in self.z_copies(f):
                out().wait_send()


def dot(a, b, ca, cb):
    return lax.dot_general(a, b, (((ca,), (cb,)), ((), ())), preferred_element_type=F32)


def parts(nz, nj, chunks, units):
    ne, nq = 2 * nj, nz // QUAD
    high, tall = ne * QUAD * CAP, QUAD * LANES
    rows = nj * nz * CAP
    out = {}
    out["meta"] = [pltpu.VMEM((nz, 16, LANES), F32), DMA((1, nz)), DMA((1, nz))]
    out["heads"] = [pltpu.VMEM((4, 8, chunks * LANES), BF16), DMA((4,)), DMA((4,))]
    for name in ("squares", "logits", "slopes"):
        out[name] = [pltpu.VMEM((4, 8, LANES), F32), DMA((4,)), DMA((4,))]
    out["picks"] = [pltpu.VMEM((nq, high, tall), BF16), pltpu.VMEM((nq, high, LANES), BF16)]
    out["places"] = [pltpu.VMEM((nq, tall, high), BF16)] * 3
    out["tokens"] = Dispatch.scratch(nz, nj, chunks)
    out["grads"] = Dispatch.scratch(nz, nj, chunks)
    out["small"] = Dispatch.scratch(nz, nj, 1)
    out["tokens_y"] = [pltpu.VMEM((nj, nz * CAP, 4 * chunks * LANES), BF16)] + Gather.scratch(chunks)
    out["grads_y"] = [pltpu.VMEM((nj, nz * CAP, 4 * chunks * LANES), BF16)] + Gather.scratch(chunks)
    out["value"] = [pltpu.VMEM((nj, nz * CAP, 4 * chunks * LANES), BF16)]
    out["forth"] = Combine.scratch(nz, nj, chunks)
    out["back"] = Combine.scratch(nz, nj, chunks)
    out["hidden"] = [pltpu.VMEM((rows, units), F32)] * 3 + [pltpu.VMEM((units, rows), BF16)]
    out["rows"] = [pltpu.VMEM((LANES, chunks * LANES), F32)] * 2
    return out


def block_kernel(nz, nj, chunks, hidden_ref, gain_ref, own_ref, later_ref, head_ref, labels_ref,
                 gate_ref, up_ref, down_ref, outcome_ref, loss_ref, grad_ref, ggate_ref, gup_ref, gdown_ref,
                 *scratch):
    groups, at = {}, 0
    for name, spec in parts(nz, nj, chunks, gate_ref.shape[0]).items():
        groups[name] = scratch[at : at + len(spec)]
        at += len(spec)
    z, j, t = place(nj)
    ne = 2 * nj
    width = 4 * chunks * LANES
    meta_ref, meta_ss, meta_rs = groups["meta"]
    heads_ref, heads_ss, heads_rs = groups["heads"]
    pick_ref, weights_ref = groups["picks"]
    (value_ref,) = groups["value"]
    gpre_ref, upre_ref, dact_ref, turned_ref = groups["hidden"]
    dout_ref, scaled_ref = groups["rows"]
    tokens = Dispatch(nz, nj, chunks, pick_ref, None, None, groups["tokens"])
    grads = Dispatch(nz, nj, chunks, pick_ref, None, None, groups["grads"])
    small = Dispatch(nz, nj, 1, pick_ref, weights_ref, lax.div(t, 2), groups["small"])
    tokens_y = Gather(chunks, tokens.r.xrecv, groups["tokens_y"][0], groups["tokens_y"][1:])
    grads_y = Gather(chunks, grads.r.xrecv, groups["grads_y"][0], groups["grads_y"][1:])
    forth = Combine(nz, nj, chunks, value_ref, groups["places"][:2], groups["forth"])
    back = Combine(nz, nj, chunks, value_ref, groups["places"][2:], groups["back"])

    enter(nz, nj)
    squares = Exchange(*groups["squares"])
    hidden = hidden_ref[...].astype(F32)
    squares.start(to_row(jnp.sum(hidden * hidden, axis=1, keepdims=True)))
    along = Along(nz, "z", nj, meta_ss, meta_rs)

    def meta_copies():
        return along.copies(0, lambda to: own_ref, lambda zz: meta_ref.at[zz])

    for out, _ in meta_copies():
        out().start()
    meta_ref[z] = own_ref[...]

    def head_copies():
        for k in range(1, 4):
            to = lax.rem(t + k, 4)
            yield (
                later(head_ref, heads_ref.at[t], heads_ss.at[k], heads_rs.at[t], {"tp": to}),
                later(head_ref, heads_ref.at[to], heads_ss.at[k], heads_rs.at[to], {"tp": to}),
            )

    inv = lax.rsqrt(to_columns(squares.total()[0:1, :]) / width + EPS)
    for f in range(chunks):
        normed = hidden_ref[:, lanes(f)].astype(F32) * inv * gain_ref[0:1, lanes(f)]
        tokens.z_send(f, normed.astype(BF16))
    for f in range(chunks):
        grads.z_send(f, later_ref[:, lanes(f)])
    for out, _ in head_copies():
        out().start()
    heads_ref[t] = head_ref[...]
    for _, arriving in meta_copies():
        arriving().wait_recv()
    build_pick(meta_ref, z, nz, ne, pick_ref, weights_ref)
    for step in range(chunks + 2):
        if step < chunks:
            tokens.pick(step)
        if 0 <= step - 1 < chunks:
            tokens.x_wait(step - 1)
            tokens_y.send(step - 1)
        if 0 <= step - 2 < chunks:
            tokens_y.forward(step - 2)
        if step == chunks - 1:
            build_place(meta_ref, z, nz, ne, *groups["places"])
    for f in range(chunks):
        tokens_y.wait(f)
        rows = tokens_y.chunk(f)
        gate = dot(rows, weight_chunk(gate_ref, f, chunks), 1, 1)
        up = dot(rows, weight_chunk(up_ref, f, chunks), 1, 1)
        if f:
            gate = gate + gpre_ref[...]
            up = up + upre_ref[...]
        gpre_ref[...] = gate
        upre_ref[...] = up
        if f < chunks - 1:
            grads.pick(f)
    gate, up = gpre_ref[...], upre_ref[...]
    active = gate * jax.nn.sigmoid(gate) * up
    active_low = active.astype(BF16)
    for f in range(chunks):
        forth.put(f, dot(active_low, weight_chunk(down_ref, f, chunks), 1, 0).astype(BF16))
    turned_ref[...] = jnp.transpose(active).astype(BF16)
    grads.pick(chunks - 1)
    for _, arriving in head_copies():
        arriving().wait_recv()
    early = chunks // 2
    for step in range(chunks + 2):
        if step < chunks:
            forth.y_sum(step)
        if step == chunks - 1:
            for f in range(early):
                grads.x_wait(f)
                grads_y.send(f)
        if 0 <= step - 1 < chunks:
            forth.x_send(step - 1)
        if 0 <= step - 2 < chunks:
            forth.mix(step - 2)
    for f in range(early):
        grads_y.forward(f)
    logits = jnp.zeros((8, LANES), F32)
    for f in range(chunks):
        outcome = (hidden_ref[:, lanes(f)].astype(F32) + forth.result(f)).astype(BF16)
        outcome_ref[:, lanes(f)] = outcome
        logits = logits + dot(head_ref[:, lanes(f)], outcome, 1, 1)
    sums = Exchange(*groups["logits"])
    sums.start(logits)
    for f in range(early, chunks):
        grads.x_wait(f)
        grads_y.send(f)
    logits = sums.total()
    row = lax.broadcasted_iota(jnp.int32, (8, LANES), 0)
    live = row < LABELS
    hot = jnp.where(row == labels_ref[0:1, :], 1.0, 0.0)
    powers = jnp.where(live, jnp.exp(jnp.where(live, logits, 0.0)), 0.0)
    totals = jnp.sum(powers, axis=0, keepdims=True)
    loss = jnp.log(totals) - jnp.sum(logits * hot, axis=0, keepdims=True)
    loss_ref[...] = jnp.broadcast_to(loss, (8, LANES))
    d_logits = (powers / totals - hot) * LOSS_SCALE
    pieces = [part.astype(F32)[0:LABELS] for part in split(d_logits, 3)]
    d_logits = jnp.concatenate(pieces + [jnp.zeros((LANES - 3 * LABELS, LANES), F32)], axis=0)
    d_logits = jnp.transpose(d_logits)
    small.z_send(0, d_logits.astype(BF16))
    head_rows = [heads_ref[s, 0:LABELS, :].astype(F32) for s in range(4)]
    blank = jnp.zeros((LANES - 3 * LABELS, chunks * LANES), F32)
    head_rows = [jnp.concatenate([rows, rows, rows, blank], axis=0).astype(BF16) for rows in head_rows]
    for f in range(chunks):
        term = jnp.zeros((LANES, LANES), F32)
        for label in range(LABELS):
            weight = head_ref[label : label + 1, lanes(f)].astype(F32)
            value = (d_logits[:, label : label + 1] + d_logits[:, LABELS + label : LABELS + label + 1]) + (
                d_logits[:, 2 * LABELS + label : 2 * LABELS + label + 1]
            )
            term = term + value * weight
        dout_ref[:, lanes(f)] = term + later_ref[:, lanes(f)].astype(F32)
    small.pick(0)
    for f in range(early, chunks):
        grads_y.forward(f)
    small.x_wait(0)
    tall = nj * nz * CAP
    slim = small.r.xrecv[0, lax.div(t, 2)].reshape(tall, LANES)
    weight = jnp.sum(slim[:, 3 * LABELS : 3 * LABELS + 3].astype(F32), axis=1, keepdims=True)
    for f in range(chunks):
        grads_y.wait(f)
        heads = jnp.concatenate([rows[:, lanes(f)] for rows in head_rows], axis=1)
        rounded = (dot(slim, heads, 1, 0) + grads_y.chunk(f).astype(F32)).astype(BF16)
        scaled = (weight * rounded.astype(F32)).astype(BF16)
        grads_y.relayed(f)
        for s in range(4):
            grads_y.out[:, :, wide(s, f, chunks)] = scaled[:, lanes(s)].reshape(nj, nz * CAP, LANES)
        part = dot(scaled, weight_chunk(down_ref, f, chunks), 1, 1)
        dact_ref[...] = part if f == 0 else dact_ref[...] + part
    gate, up, d_active = gpre_ref[...], upre_ref[...], dact_ref[...]
    sigma = jax.nn.sigmoid(gate)
    d_gate = d_active * up * sigma * (1.0 + gate * (1.0 - sigma))
    d_up = d_active * gate * sigma
    gpre_ref[...] = d_gate
    upre_ref[...] = d_up
    d_gate, d_up = d_gate.astype(BF16), d_up.astype(BF16)
    forth.sent()
    for f in range(chunks):
        total = dot(d_gate, weight_chunk(gate_ref, f, chunks), 1, 0)
        total = total + dot(d_up, weight_chunk(up_ref, f, chunks), 1, 0)
        back.put(f, total.astype(BF16))

    def weight_grad(left, right, out):
        def one(i, carry):
            where = pl.ds(pl.multiple_of(i * 2 * LANES, 2 * LANES), 2 * LANES)
            got = right[:, :, where].reshape(tall, 2 * LANES)
            out[:, where] = jnp.dot(left[...], got, preferred_element_type=F32).astype(BF16)
            return carry

        lax.fori_loop(0, width // (2 * LANES), one, 0)

    weight_grad(turned_ref, grads_y.out, gdown_ref)
    turned_ref[...] = jnp.transpose(gpre_ref[...]).astype(BF16)
    weight_grad(turned_ref, tokens_y.out, ggate_ref)
    turned_ref[...] = jnp.transpose(upre_ref[...]).astype(BF16)
    weight_grad(turned_ref, tokens_y.out, gup_ref)
    for step in range(chunks + 2):
        if step < chunks:
            back.y_sum(step)
        if 0 <= step - 1 < chunks:
            back.x_send(step - 1)
        if 0 <= step - 2 < chunks:
            back.mix(step - 2)
    slope = jnp.zeros((LANES, LANES), F32)
    for f in range(chunks):
        scaled = back.result(f) * gain_ref[0:1, lanes(f)]
        scaled_ref[:, lanes(f)] = scaled
        slope = slope + scaled * hidden_ref[:, lanes(f)].astype(F32)
    slopes = Exchange(*groups["slopes"])
    slopes.start(to_row(jnp.sum(slope, axis=1, keepdims=True)))
    slope = to_columns(slopes.total()[0:1, :]) / width
    inv = lax.rsqrt(to_columns(squares.total_again()[0:1, :]) / width + EPS)
    cube = inv * inv * inv
    for f in range(chunks):
        d_hidden = inv * scaled_ref[:, lanes(f)] - hidden_ref[:, lanes(f)].astype(F32) * cube * slope
        grad_ref[:, lanes(f)] = (dout_ref[:, lanes(f)] + d_hidden).astype(BF16)
    back.sent()
    for f in range(chunks):
        tokens_y.relayed(f)
    for copies in (meta_copies, head_copies):
        for out, _ in copies():
            out().wait_send()
    for part in (squares, sums, slopes, tokens, grads, small, tokens_y, grads_y, forth, back):
        part.drain()


def shards(nz, nj, hidden_in, norm_gain, expert_ids, routing_weight, labels, grad_later, head_weight,
           gate_weight, up_weight, down_weight):
    chunks = hidden_in.shape[1] // LANES
    vmem = pl.BlockSpec(memory_space=pltpu.VMEM)
    own = jnp.concatenate([expert_ids.T.astype(F32), routing_weight.T], axis=0)
    head = jnp.concatenate([head_weight.T, jnp.zeros_like(head_weight.T)], axis=0)
    args = (hidden_in, norm_gain[None, :], own, grad_later, head, labels[None, :],
            gate_weight, up_weight, down_weight)
    outs = [
        jax.ShapeDtypeStruct(hidden_in.shape, BF16),
        jax.ShapeDtypeStruct((8, LANES), F32),
        jax.ShapeDtypeStruct(hidden_in.shape, BF16),
    ] + [jax.ShapeDtypeStruct(gate_weight.shape, BF16)] * 3
    scratch = [spec for group in parts(nz, nj, chunks, gate_weight.shape[0]).values() for spec in group]
    outcome, loss, grad_input, grad_gate, grad_up, grad_down = pl.pallas_call(
        functools.partial(block_kernel, nz, nj, chunks),
        out_shape=outs,
        in_specs=[vmem] * len(args),
        out_specs=[vmem] * len(outs),
        scratch_shapes=scratch,
        name="expert_block",
        compiler_params=pltpu.CompilerParams(
            collective_id=1, has_side_effects=True, vmem_limit_bytes=67043328
        ),
    )(*args)
    return loss[0], outcome, grad_input, grad_gate, grad_up, grad_down


def solution(mesh, nj=8):
    nz = mesh.shape["ep"] // nj
    in_specs = (
        P("ep", "tp"),
        P("tp"),
        P("ep", None),
        P("ep", None),
        P("ep"),
        P("ep", "tp"),
        P("tp", None),
        P(("ep", "tp"), None),
        P(("ep", "tp"), None),
        P(("ep", "tp"), None),
    )
    out_specs = (
        P("ep"),
        P("ep", "tp"),
        P("ep", "tp"),
        P(("ep", "tp"), None),
        P(("ep", "tp"), None),
        P(("ep", "tp"), None),
    )
    return jax.shard_map(
        functools.partial(shards, nz, nj), mesh=mesh, in_specs=in_specs, out_specs=out_specs, check_vma=False
    )
```
